32 devices in a mesh: floor: 4 (over y, x), strip: 8 (over z, core).
Axes of the slice: x: 2, y: 2, z: 4, core: 2. Of those that a mesh axis runs over, the one named last changes fastest.
Arguments:
- density: float32 [4, 4, 512, 2048], P('floor', None, 'strip'), may hold values from 0.2 to 2
- value_field: float32 [4, 4, 512, 2048], P('floor', None, 'strip'), may hold values from -3 to 3
- row_kernel: bfloat16 [512, 512], P('strip'), may hold values from -0.25 to 0.25
- column_kernel: bfloat16 [2048, 2048], replicated, may hold values from -0.125 to 0.125
- type_weight: float32 [4], replicated, may hold values from 0.5 to 2
- crowd_cost: float32 [4], replicated, may hold values from 0.1 to 1
- exit_drain: float32 [4], replicated, may hold values from 0.05 to 0.5
- exit_type: int32 [4, 128], P('floor', 'strip'), may hold values from 0 to 7
- landing_map: int32 [4, 64, 4], P(None, 'strip'), may hold values from 0 to 63, as said below
Outputs:
- final_density: float32 [4, 4, 512, 2048], P('floor', None, 'strip')
- final_value: float32 [4, 4, 512, 2048], P('floor', None, 'strip')
The draws below stay inside these ranges and needn't reach their ends.
Inputs may be any that keep to these rules, and one draw needn't show every extreme that they name: Each row of landing_map[f] gives a landing's source tile and source face row on floor f and its target tile and target face row on floor f - 1, in the same strip; tiles lie below 16 and face rows below 64, counted within the strip. Every strip of a floor has 8 landings, with distinct sources and distinct targets. `exit_type`: A value below 4 makes the tile an exit target of that occupant type; larger values mark tiles with no target.
All inputs are finite; a program needn't handle non-finite values.
Results may differ from the reference program's by a relative error of at most 0.0026.
Values may be sent and summed in bfloat16 or wider, within the bound.
A program may use at most 128 MiB of HBM per device.

```python
import math
import jax
import jax.numpy as jnp
from jax import lax

COLS = 2048
TYPES = 4
ROWS_DEV = 64
SUBSTEPS = 4
TILES = 16
LANDINGS = 8
FLOORS = 4
FLOOR_ROWS = 512
N_STRIP = 8


def draw_landing_map(key, part):
    cells = TILES * ROWS_DEV
    blocks = FLOORS * N_STRIP
    keys = jax.random.split(key, 2 * blocks)

    def pick(one_key):
        return jax.random.permutation(one_key, cells - 1)[:LANDINGS]
    chosen = jax.vmap(pick)(keys).astype(jnp.int32)
    block_ids = jnp.arange(2 * blocks, dtype=jnp.int32)
    slot_ids = jnp.arange(LANDINGS, dtype=jnp.int32)
    forced = (block_ids[:, None] % blocks == 0) & (slot_ids[None, :] == LANDINGS - 1)
    chosen = jnp.where(forced, jnp.int32(cells - 1), chosen)
    chosen = chosen.reshape(2, FLOORS, N_STRIP * LANDINGS)
    tile_index = chosen // ROWS_DEV
    row_index = chosen % ROWS_DEV
    return jnp.stack([tile_index[0], row_index[0], tile_index[1], row_index[1]], axis=-1)


def set_ends(drawn, stream_key, least, largest):
    index_at = [jax.random.randint(jax.random.fold_in(stream_key, axis), (), 0, length) for axis, length in enumerate(drawn.shape)]
    widest = drawn.shape.index(max(drawn.shape))
    neighbour = index_at[:widest] + [(index_at[widest] + 1) % drawn.shape[widest]] + index_at[widest + 1:]
    return drawn.at[tuple(index_at)].set(least).at[tuple(neighbour)].set(largest)


def shard_levels(own_key, shape, pieces, low, top_value):
    loudness, own = 1.0, jax.random.fold_in(own_key, 6)
    for position, parts in pieces:
        heights = jnp.exp(jax.random.uniform(jax.random.fold_in(own, position), (parts,), jnp.float32, low / len(pieces), top_value / len(pieces)))
        loudness = loudness * jnp.repeat(heights, shape[position] // parts).reshape([-1 if axis == position else 1 for axis in range(len(shape))])
    return loudness


def noise(rng, dims, scale, most, cuts=(), kind=jnp.bfloat16):
    drawn = scale * jax.random.normal(rng, dims, jnp.float32)
    if cuts:
        drawn = drawn * shard_levels(rng, dims, cuts, -0.22, 0.18)
    return jnp.clip(drawn, -most, most).astype(kind)


def setup_inputs(seed: int = 0) -> dict:
    arg_keys = jax.random.split(jax.random.key(seed), 10)
    return {
        "density": jnp.clip(jnp.exp(math.log(2.0) - 2.3025851 * jax.random.uniform(arg_keys[0], (FLOORS, TYPES, FLOOR_ROWS, COLS), jnp.float32) ** shard_levels(arg_keys[0], (FLOORS, TYPES, FLOOR_ROWS, COLS), ((0, 4), (2, 8)), -0.2, 0.2)), 0.2, 2.0),
        "value_field": noise(arg_keys[1], (FLOORS, TYPES, FLOOR_ROWS, COLS), 0.5, 3.0, ((0, 4), (2, 8)), jnp.float32),
        "row_kernel": noise(arg_keys[2], (FLOOR_ROWS, FLOOR_ROWS), FLOOR_ROWS ** -0.5, 0.25, ((0, 8),)),
        "column_kernel": noise(arg_keys[3], (COLS, COLS), COLS ** -0.5, 0.125),
        "type_weight": jnp.clip(jnp.exp(jax.random.uniform(arg_keys[4], (TYPES,), jnp.float32, math.log(0.5), math.log(2.0))), 0.5, 2.0),
        "crowd_cost": jnp.clip(jnp.exp(jax.random.uniform(arg_keys[5], (TYPES,), jnp.float32, math.log(0.1), math.log(1.0))), 0.1, 1.0),
        "exit_drain": jnp.clip(jnp.exp(jax.random.uniform(arg_keys[6], (TYPES,), jnp.float32, math.log(0.05), math.log(0.5))), 0.05, 0.5),
        "exit_type": set_ends(jax.random.randint(arg_keys[7], (FLOORS, N_STRIP * TILES), 0, 2 * TYPES), jax.random.fold_in(arg_keys[7], 1), 0, (2 * TYPES) - 1).astype(jnp.int32),
        "landing_map": draw_landing_map(jax.random.fold_in(arg_keys[9], 71), 0),
    }


time_step = 0.2
viscosity = 1.0
exit_reward = 2.0
stair_rate = 0.5


def advance(padded, crowd_cost, exit_drain, potential, target):
    types = crowd_cost.shape[0]
    dens_pad = padded[:types]
    val_pad = padded[types:]
    dens_now = dens_pad[:, 1:-1, 1:-1]
    value_now = val_pad[:, 1:-1, 1:-1]
    dens_near = (dens_pad[:, 2:, 1:-1], dens_pad[:, :-2, 1:-1], dens_pad[:, 1:-1, 2:], dens_pad[:, 1:-1, :-2])
    val_near = (val_pad[:, 2:, 1:-1], val_pad[:, :-2, 1:-1], val_pad[:, 1:-1, 2:], val_pad[:, 1:-1, :-2])
    laplace_value = val_near[0] + val_near[1] + val_near[2] + val_near[3] - 4.0 * value_now
    laplace_dens = dens_near[0] + dens_near[1] + dens_near[2] + dens_near[3] - 4.0 * dens_now
    grad_rows = 0.5 * (val_near[0] - val_near[1])
    grad_cols = 0.5 * (val_near[2] - val_near[3])
    flux_sum = 0.5 * (dens_near[0] + dens_now) * (val_near[0] - value_now) - 0.5 * (dens_now + dens_near[1]) * (value_now - val_near[1])
    flux_sum = flux_sum + 0.5 * (dens_near[2] + dens_now) * (val_near[2] - value_now) - 0.5 * (dens_now + dens_near[3]) * (value_now - val_near[3])
    new_value = value_now + time_step * (viscosity * laplace_value - 0.5 * (grad_rows * grad_rows + grad_cols * grad_cols) + crowd_cost[:, None, None] * potential[None] - exit_reward * target)
    moved = dens_now + time_step * (viscosity * laplace_dens + flux_sum)
    drained = moved * (1.0 - exit_drain[:, None, None] * target)
    return drained, new_value


def reference(density, value_field, row_kernel, column_kernel, type_weight, crowd_cost, exit_drain, exit_type, landing_map):
    tile_cols = COLS // TILES
    type_range = jnp.arange(TYPES, dtype=jnp.int32)
    tiles_all = exit_type.reshape(FLOORS, N_STRIP, TILES)
    target_small = (tiles_all[:, None, :, :] == type_range[None, :, None, None]).astype(jnp.float32)

    def floor_step(inputs):
        dens_now, value_now, small = inputs
        target = jnp.repeat(jnp.repeat(small, ROWS_DEV, axis=1), tile_cols, axis=2)
        crowd = jnp.sum(type_weight[:, None, None] * dens_now, axis=0).astype(jnp.bfloat16)
        mixed = jnp.dot(row_kernel, crowd, preferred_element_type=jnp.float32).astype(jnp.bfloat16)
        potential = jnp.dot(mixed, column_kernel, preferred_element_type=jnp.float32)
        stacked = jnp.concatenate([dens_now, value_now], axis=0)
        padded = jnp.pad(stacked, ((0, 0), (1, 1), (1, 1)), mode="edge")
        return advance(padded, crowd_cost, exit_drain, potential, target)

    strip_base = (jnp.arange(N_STRIP * LANDINGS, dtype=jnp.int32) // LANDINGS) * ROWS_DEV
    src_tile = landing_map[:, :, 0]
    src_row = landing_map[:, :, 1] + strip_base[None, :]
    dst_tile = landing_map[:, :, 2]
    dst_row = landing_map[:, :, 3] + strip_base[None, :]
    dst_tile_next = jnp.concatenate([dst_tile[1:], dst_tile[-1:]], axis=0)
    dst_row_next = jnp.concatenate([dst_row[1:], dst_row[-1:]], axis=0)

    def take_rows(view_floor, row_index, tile_index):
        return view_floor[:, row_index, tile_index, :]

    def place_rows(view_floor, row_src, tile_src, outflow, row_dst, tile_dst, incoming):
        view_floor = view_floor.at[:, row_src, tile_src, :].add(-outflow)
        return view_floor.at[:, row_dst, tile_dst, :].add(incoming)

    for substep in range(SUBSTEPS):
        drained, value_field = lax.map(floor_step, (density, value_field, target_small))
        view = drained.reshape(FLOORS, TYPES, FLOOR_ROWS, TILES, tile_cols)
        outflow = stair_rate * jax.vmap(take_rows)(view, src_row, src_tile)
        incoming = jnp.concatenate([outflow[1:], jnp.zeros_like(outflow[:1])], axis=0)
        view = jax.vmap(place_rows)(view, src_row, src_tile, outflow, dst_row_next, dst_tile_next, incoming)
        density = view.reshape(FLOORS, TYPES, FLOOR_ROWS, COLS)
    return density, value_field
```

```python
import functools

import jax
import jax.numpy as jnp
from jax import lax
from jax.experimental import pallas as pl
from jax.experimental.pallas import tpu as pltpu
from jax.sharding import PartitionSpec as P

SUBSTEPS = 4
TILES = 16
LANE = 128
TOP = 8
BLOCK = 512

time_step = 0.2
viscosity = 1.0
exit_reward = 2.0
stair_rate = 0.5

MESH = pl.DeviceIdType.MESH


def kernel(
    strips, floors, landings, types, rows, width,
    dens_hbm, val_hbm, rk_ref, ck_hbm, tw_ref, cc_ref, ed_ref, et_ref, lm_ref,
    dens_out, val_out,
    m_buf, u_buf, ck, rk, crowd_send, crowd_recv, mix_send, mix_recv,
    hm_send, hm_recv, hu_send, hu_recv, out_send, out_recv,
    drain_fac, reward, keep_map, dst_map, faces,
    load_sem, store_sem, rk_ssem, rk_rsem, c_ssem, c_rsem, x_ssem, x_rsem,
    hm_ssem, hm_rsem, hu_ssem, hu_rsem, o_ssem, o_rsem,
):
    me = lax.axis_index("strip")
    floor = lax.axis_index("floor")
    cw = width // strips
    tile_cols = width // TILES
    per = cw // LANE
    inner = pl.ds(TOP, rows)
    cols = pl.ds(LANE, width)

    load_m = pltpu.make_async_copy(dens_hbm.at[0], m_buf.at[0, :, inner, cols], load_sem.at[0])
    load_u = pltpu.make_async_copy(val_hbm.at[0], u_buf.at[0, :, inner, cols], load_sem.at[1])
    load_ck = pltpu.make_async_copy(ck_hbm, ck, load_sem.at[2])
    load_m.start()
    load_u.start()
    load_ck.start()

    barrier = pltpu.get_barrier_semaphore()
    for off in range(1, strips):
        pl.semaphore_signal(barrier, inc=1, device_id={"strip": lax.rem(me + off, strips)}, device_id_type=MESH)

    @pl.when(floor > 0)
    def _():
        pl.semaphore_signal(barrier, inc=1, device_id={"floor": floor - 1}, device_id_type=MESH)

    @pl.when(floor < floors - 1)
    def _():
        pl.semaphore_signal(barrier, inc=1, device_id={"floor": floor + 1}, device_id_type=MESH)

    peers = strips - 1 + jnp.where(floor > 0, 1, 0) + jnp.where(floor < floors - 1, 1, 0)
    pl.semaphore_wait(barrier, peers)

    def to_all(src_of, dst_ref, ssem, rsem):
        for off in range(1, strips):
            dst = lax.rem(me + off, strips)
            pltpu.make_async_remote_copy(
                src_ref=src_of(dst), dst_ref=dst_ref.at[me],
                send_sem=ssem.at[off], recv_sem=rsem.at[off],
                device_id={"strip": dst}, device_id_type=MESH,
            ).start()

    def from_all(src_of, dst_ref, ssem, rsem):
        for off in range(1, strips):
            dst = lax.rem(me + off, strips)
            src = lax.rem(me + strips - off, strips)
            pltpu.make_async_remote_copy(
                src_ref=src_of(dst), dst_ref=dst_ref.at[src],
                send_sem=ssem.at[off], recv_sem=rsem.at[off],
                device_id={"strip": dst}, device_id_type=MESH,
            ).wait()

    def rim_copy(send, recv, ssem, rsem, t, side):
        return pltpu.make_async_remote_copy(
            src_ref=send.at[t, side], dst_ref=recv.at[t, 1 - side],
            send_sem=ssem.at[t, side], recv_sem=rsem.at[t, 1 - side],
            device_id={"strip": me - 1 if side == 0 else me + 1}, device_id_type=MESH,
        )

    def send_rims(buf, send, recv, ssem, rsem, t):
        for k in range(types):
            send[t, 0, k:k + 1, :] = buf[t % 2, k, TOP:TOP + 1, cols]
            send[t, 1, k:k + 1, :] = buf[t % 2, k, TOP + rows - 1:TOP + rows, cols]

        @pl.when(me > 0)
        def _():
            rim_copy(send, recv, ssem, rsem, t, 0).start()

        @pl.when(me < strips - 1)
        def _():
            rim_copy(send, recv, ssem, rsem, t, 1).start()

    def take_rims(buf, send, recv, ssem, rsem, t):
        def own(side):
            at = TOP if side == 0 else TOP + rows - 1
            to = TOP - 1 if side == 0 else TOP + rows
            for k in range(types):
                buf[t % 2, k, to:to + 1, cols] = buf[t % 2, k, at:at + 1, cols]

        def got(side):
            c = rim_copy(send, recv, ssem, rsem, t, side)
            c.wait_send()
            pltpu.make_async_remote_copy(
                src_ref=send.at[t, side], dst_ref=recv.at[t, side],
                send_sem=ssem.at[t, side], recv_sem=rsem.at[t, side],
                device_id={"strip": me - 1 if side == 0 else me + 1}, device_id_type=MESH,
            ).wait_recv()
            to = TOP - 1 if side == 0 else TOP + rows
            for k in range(types):
                buf[t % 2, k, to:to + 1, cols] = recv[t, side, k:k + 1, :]

        pl.when(me > 0)(lambda: got(0))
        pl.when(me == 0)(lambda: own(0))
        pl.when(me < strips - 1)(lambda: got(1))
        pl.when(me == strips - 1)(lambda: own(1))

    def pad_cols(buf, b):
        for k in range(types):
            first = buf[b, k, inner, LANE:2 * LANE]
            last = buf[b, k, inner, width:width + LANE]
            buf[b, k, inner, 0:LANE] = pltpu.roll(first, LANE - 1, 1)
            buf[b, k, inner, width + LANE:width + 2 * LANE] = pltpu.roll(last, 1, 1)

    def crowd_of(t, initial):
        b = t % 2

        @pl.loop(0, strips)
        def _(j):
            for q in range(per):
                start = pl.multiple_of(j * cw + q * LANE, LANE)
                at = pl.ds(pl.multiple_of(start + LANE, LANE), LANE)
                total = None
                if not initial:
                    keep = keep_map[:, pl.ds(start, LANE)]
                    ids = dst_map[:, pl.ds(start, LANE)]
                for k in range(types):
                    v = m_buf[b, k, inner, at]
                    if not initial:
                        add = jnp.zeros_like(v)
                        for l in range(landings):
                            add = jnp.where(ids == l, out_recv[t - 1, k, l:l + 1, :], add)
                        v = v * keep + add
                        m_buf[b, k, inner, at] = v
                    term = tw_ref[k] * v
                    total = term if total is None else total + term
                if t < SUBSTEPS:
                    crowd_send[t, j, :, q * LANE:(q + 1) * LANE] = total.astype(jnp.bfloat16)

    def send_crowd(t):
        to_all(lambda d: crowd_send.at[t, d], crowd_recv.at[t], c_ssem.at[t], c_rsem.at[t])
        crowd_recv[t, me] = crowd_send[t, me]

    def mix(t):
        from_all(lambda d: crowd_send.at[t, d], crowd_recv.at[t], c_ssem.at[t], c_rsem.at[t])
        crowd = crowd_recv[t].reshape(strips * rows, cw)

        @pl.loop(0, strips)
        def _(j):
            mix_send[t, j] = jnp.dot(rk[j], crowd, preferred_element_type=jnp.float32).astype(jnp.bfloat16)

        to_all(lambda d: mix_send.at[t, d], mix_recv.at[t], x_ssem.at[t], x_rsem.at[t])
        mix_recv[t, me] = mix_send[t, me]

    def add_potential(t):
        b = (t + 1) % 2
        from_all(lambda d: mix_send.at[t, d], mix_recv.at[t], x_ssem.at[t], x_rsem.at[t])
        step = 2 * LANE

        @pl.loop(0, width // step)
        def _(n):
            start = pl.multiple_of(n * step, step)
            acc = None
            for s in range(strips):
                d = jnp.dot(mix_recv[t, s], ck[s * cw:(s + 1) * cw, pl.ds(start, step)], preferred_element_type=jnp.float32)
                acc = d if acc is None else acc + d
            at = pl.ds(pl.multiple_of(start + LANE, LANE), step)
            for k in range(types):
                u_buf[b, k, inner, at] = u_buf[b, k, inner, at] + (time_step * cc_ref[k]) * acc

    def stencil(t):
        b, nb = t % 2, (t + 1) % 2

        @pl.loop(0, types * (width // BLOCK))
        def _(i):
            k = lax.div(i, width // BLOCK)
            start = pl.multiple_of(lax.rem(i, width // BLOCK) * BLOCK, BLOCK)
            wide = pl.ds(start, BLOCK + 2 * LANE)
            mid = pl.ds(pl.multiple_of(start + LANE, LANE), BLOCK)
            fac = drain_fac[k, :, pl.ds(start, BLOCK)]
            rew = reward[k, :, pl.ds(start, BLOCK)]
            for r in range(rows // 8):
                lo = TOP + 8 * r
                mw = m_buf[b, k, lo:lo + 8, wide]
                uw = u_buf[b, k, lo:lo + 8, wide]
                span = BLOCK + 2 * LANE
                m = mw[:, LANE:-LANE]
                u = uw[:, LANE:-LANE]
                ml = pltpu.roll(mw, 1, 1)[:, LANE:-LANE]
                mr = pltpu.roll(mw, span - 1, 1)[:, LANE:-LANE]
                ul = pltpu.roll(uw, 1, 1)[:, LANE:-LANE]
                ur = pltpu.roll(uw, span - 1, 1)[:, LANE:-LANE]
                mu = m_buf[b, k, lo - 1:lo + 7, mid]
                md = m_buf[b, k, lo + 1:lo + 9, mid]
                uu = u_buf[b, k, lo - 1:lo + 7, mid]
                ud = u_buf[b, k, lo + 1:lo + 9, mid]
                flux = None
                lap_u = None
                for mn, un in ((mu, uu), (md, ud), (ml, ul), (mr, ur)):
                    d = un - u
                    term = viscosity * (mn - m) + (mn + m) * (0.5 * d)
                    flux = term if flux is None else flux + term
                    lap_u = d if lap_u is None else lap_u + d
                gr = ud - uu
                gc = ur - ul
                drained = (m + time_step * flux) * fac
                m_buf[nb, k, lo:lo + 8, mid] = drained
                for q in range(BLOCK // LANE):
                    faces[(lax.div(start, LANE) + q) * (rows // 8) + r, k] = drained[:, q * LANE:(q + 1) * LANE]
                u_buf[nb, k, lo:lo + 8, mid] = u + (time_step * viscosity) * lap_u - (0.125 * time_step) * (gr * gr + gc * gc) - rew

    def out_copy(t):
        return pltpu.make_async_remote_copy(
            src_ref=out_send.at[t], dst_ref=out_recv.at[t],
            send_sem=o_ssem.at[t], recv_sem=o_rsem.at[t],
            device_id={"floor": floor - 1}, device_id_type=MESH,
        )

    def stairs(t):
        nb = (t + 1) % 2
        for l in range(landings):
            row = lm_ref[floor, l, 1]
            group = lax.div(row, 8)
            hit = eight + 8 * group == row
            face = faces[lm_ref[floor, l, 0] * (rows // 8) + group]
            out_send[t, :, l, :] = stair_rate * jnp.sum(jnp.where(hit, face, 0.0), axis=1)

        @pl.when(floor > 0)
        def _():
            out_copy(t).start()

    def stairs_in(t):
        @pl.when(floor > 0)
        def _():
            out_copy(t).wait_send()

        @pl.when(floor < floors - 1)
        def _():
            out_copy(t).wait_recv()

        @pl.when(floor == floors - 1)
        def _():
            out_recv[t] = jnp.zeros_like(out_recv[t])

    hm = (hm_send, hm_recv, hm_ssem, hm_rsem)
    hu = (hu_send, hu_recv, hu_ssem, hu_rsem)

    load_m.wait()
    crowd_of(0, True)
    send_crowd(0)
    send_rims(m_buf, *hm, 0)
    load_u.wait()
    send_rims(u_buf, *hu, 0)
    to_all(lambda d: rk_ref, rk, rk_ssem, rk_rsem)
    rk[me] = rk_ref[...]

    above = jnp.minimum(floor + 1, floors - 1)
    for tile in range(TILES):
        kind = et_ref[0, tile]
        here = slice(tile * tile_cols, (tile + 1) * tile_cols)
        for k in range(types):
            hit = jnp.where(kind == k, 1.0, 0.0).astype(jnp.float32)
            drain_fac[k, :, here] = jnp.full((8, tile_cols), 1.0 - ed_ref[k] * hit, jnp.float32)
            reward[k, :, here] = jnp.full((8, tile_cols), (time_step * exit_reward) * hit, jnp.float32)

    eight = lax.broadcasted_iota(jnp.int32, (types, 8, LANE), 1)
    row_at = lax.broadcasted_iota(jnp.int32, (rows, LANE), 0)

    @pl.loop(0, TILES)
    def _(tile):
        keep = jnp.ones((rows, LANE), jnp.float32)
        ids = jnp.full((rows, LANE), landings, jnp.int32)
        for l in range(landings):
            src_row = jnp.where(lm_ref[floor, l, 0] == tile, lm_ref[floor, l, 1], -1)
            dst_row = jnp.where(lm_ref[above, l, 2] == tile, lm_ref[above, l, 3], -1)
            keep = jnp.where(row_at == src_row, 1.0 - stair_rate, keep)
            ids = jnp.where(row_at == dst_row, l, ids)
        at = pl.ds(pl.multiple_of(tile * LANE, LANE), LANE)
        keep_map[:, at] = keep
        dst_map[:, at] = ids

    for t in range(SUBSTEPS):
        if t > 0:
            if t == 1:
                load_ck.wait()
            add_potential(t - 1)
            send_rims(u_buf, *hu, t)
            if t >= 2:
                mix(t)
        pad_cols(m_buf, t % 2)
        pad_cols(u_buf, t % 2)
        take_rims(m_buf, *hm, t)
        take_rims(u_buf, *hu, t)
        stencil(t)
        stairs(t)
        stairs_in(t)
        crowd_of(t + 1, False)
        if t + 1 < SUBSTEPS:
            send_crowd(t + 1)
            send_rims(m_buf, *hm, t + 1)
        if t == 0:
            from_all(lambda d: rk_ref, rk, rk_ssem, rk_rsem)
            mix(0)
            mix(1)
    last = SUBSTEPS % 2
    save_m = pltpu.make_async_copy(m_buf.at[last, :, inner, cols], dens_out.at[0], store_sem.at[0])
    save_m.start()
    add_potential(SUBSTEPS - 1)
    save_u = pltpu.make_async_copy(u_buf.at[last, :, inner, cols], val_out.at[0], store_sem.at[1])
    save_u.start()
    save_m.wait()
    save_u.wait()


def solution(mesh):
    strips = mesh.shape["strip"]
    floors = mesh.shape["floor"]

    def local(density, value_field, row_kernel, column_kernel, type_weight, crowd_cost, exit_drain, exit_type, landing_map):
        _, types, rows, width = density.shape
        landings = landing_map.shape[1]
        depth = row_kernel.shape[1]
        cw = width // strips
        n = SUBSTEPS
        any_spec = pl.BlockSpec(memory_space=pl.ANY)
        vmem = pl.BlockSpec(memory_space=pltpu.VMEM)
        smem = pl.BlockSpec(memory_space=pltpu.SMEM)
        f32, bf16 = jnp.float32, jnp.bfloat16
        dma = pltpu.SemaphoreType.DMA
        return pl.pallas_call(
            functools.partial(kernel, strips, floors, landings, types, rows, width),
            out_shape=(
                jax.ShapeDtypeStruct(density.shape, f32),
                jax.ShapeDtypeStruct(value_field.shape, f32),
            ),
            in_specs=[any_spec, any_spec, vmem, any_spec, smem, smem, smem, smem, smem],
            out_specs=(any_spec, any_spec),
            scratch_shapes=[
                pltpu.VMEM((2, types, rows + 2 * TOP, width + 2 * LANE), f32),
                pltpu.VMEM((2, types, rows + 2 * TOP, width + 2 * LANE), f32),
                pltpu.VMEM(column_kernel.shape, bf16),
                pltpu.VMEM((strips, rows, depth), bf16),
                pltpu.VMEM((n, strips, rows, cw), bf16),
                pltpu.VMEM((n, strips, rows, cw), bf16),
                pltpu.VMEM((n, strips, rows, cw), bf16),
                pltpu.VMEM((n, strips, rows, cw), bf16),
                pltpu.VMEM((n, 2, types, width), f32),
                pltpu.VMEM((n, 2, types, width), f32),
                pltpu.VMEM((n, 2, types, width), f32),
                pltpu.VMEM((n, 2, types, width), f32),
                pltpu.VMEM((n, types, landings, LANE), f32),
                pltpu.VMEM((n, types, landings, LANE), f32),
                pltpu.VMEM((types, 8, width), f32),
                pltpu.VMEM((types, 8, width), f32),
                pltpu.VMEM((rows, width), f32),
                pltpu.VMEM((rows, width), jnp.int32),
                pltpu.VMEM((width // LANE * (rows // 8), types, 8, LANE), f32),
                dma((3,)),
                dma((2,)),
                dma((strips,)),
                dma((strips,)),
                dma((n, strips)),
                dma((n, strips)),
                dma((n, strips)),
                dma((n, strips)),
                dma((n, 2)),
                dma((n, 2)),
                dma((n, 2)),
                dma((n, 2)),
                dma((n,)),
                dma((n,)),
            ],
            compiler_params=pltpu.CompilerParams(
                collective_id=0, has_side_effects=True, vmem_limit_bytes=52 * 1024 * 1024
            ),
        )(density, value_field, row_kernel, column_kernel, type_weight, crowd_cost, exit_drain, exit_type, landing_map)

    placed = (
        P("floor", None, "strip", None),
        P("floor", None, "strip", None),
        P("strip", None),
        P(),
        P(),
        P(),
        P(),
        P("floor", "strip"),
        P(None, "strip", None),
    )
    return jax.shard_map(
        local,
        mesh=mesh,
        in_specs=placed,
        out_specs=(P("floor", None, "strip", None), P("floor", None, "strip", None)),
        check_vma=False,
    )
```

```python
import functools

import jax
import jax.numpy as jnp
from jax import lax
from jax.experimental import pallas as pl
from jax.experimental.pallas import tpu as pltpu
from jax.sharding import PartitionSpec as P

SUBSTEPS = 4
TILES = 16
LANE = 128
TOP = 8
BLOCK = 512

time_step = 0.2
viscosity = 1.0
exit_reward = 2.0
stair_rate = 0.5

MESH = pl.DeviceIdType.MESH


def kernel(
    strips, floors, landings, types, rows, width,
    dens_hbm, val_hbm, rk_ref, ck_hbm, tw_ref, cc_ref, ed_ref, et_ref, lm_ref,
    dens_out, val_out,
    m_buf, u_buf, ck, rk, crowd_send, crowd_recv, mix_send, mix_recv,
    hm_send, hm_recv, hu_send, hu_recv, out_send, out_recv,
    drain_fac, reward, keep_map, dst_map, faces,
    load_sem, store_sem, rk_ssem, rk_rsem, c_ssem, c_rsem, x_ssem, x_rsem,
    hm_ssem, hm_rsem, hu_ssem, hu_rsem, o_ssem, o_rsem,
):
    me = lax.axis_index("strip")
    floor = lax.axis_index("floor")
    cw = width // strips
    tile_cols = width // TILES
    per = cw // LANE
    inner = pl.ds(TOP, rows)
    cols = pl.ds(LANE, width)

    load_m = pltpu.make_async_copy(dens_hbm.at[0], m_buf.at[0, :, inner, cols], load_sem.at[0])
    load_u = pltpu.make_async_copy(val_hbm.at[0], u_buf.at[0, :, inner, cols], load_sem.at[1])
    load_ck = pltpu.make_async_copy(ck_hbm, ck, load_sem.at[2])
    load_m.start()
    load_u.start()
    load_ck.start()

    barrier = pltpu.get_barrier_semaphore()
    for off in range(1, strips):
        pl.semaphore_signal(barrier, inc=1, device_id={"strip": lax.rem(me + off, strips)}, device_id_type=MESH)

    @pl.when(floor > 0)
    def _():
        pl.semaphore_signal(barrier, inc=1, device_id={"floor": floor - 1}, device_id_type=MESH)

    @pl.when(floor < floors - 1)
    def _():
        pl.semaphore_signal(barrier, inc=1, device_id={"floor": floor + 1}, device_id_type=MESH)

    peers = strips - 1 + jnp.where(floor > 0, 1, 0) + jnp.where(floor < floors - 1, 1, 0)
    pl.semaphore_wait(barrier, peers)

    def to_all(src_of, dst_ref, ssem, rsem):
        for off in range(1, strips):
            dst = lax.rem(me + off, strips)
            pltpu.make_async_remote_copy(
                src_ref=src_of(dst), dst_ref=dst_ref.at[me],
                send_sem=ssem.at[off], recv_sem=rsem.at[off],
                device_id={"strip": dst}, device_id_type=MESH,
            ).start()

    def from_all(src_of, dst_ref, ssem, rsem):
        for off in range(1, strips):
            dst = lax.rem(me + off, strips)
            src = lax.rem(me + strips - off, strips)
            pltpu.make_async_remote_copy(
                src_ref=src_of(dst), dst_ref=dst_ref.at[src],
                send_sem=ssem.at[off], recv_sem=rsem.at[off],
                device_id={"strip": dst}, device_id_type=MESH,
            ).wait()

    def rim_copy(send, recv, ssem, rsem, t, side):
        return pltpu.make_async_remote_copy(
            src_ref=send.at[t, side], dst_ref=recv.at[t, 1 - side],
            send_sem=ssem.at[t, side], recv_sem=rsem.at[t, 1 - side],
            device_id={"strip": me - 1 if side == 0 else me + 1}, device_id_type=MESH,
        )

    def send_rims(buf, send, recv, ssem, rsem, t):
        for k in range(types):
            send[t, 0, k:k + 1, :] = buf[t % 2, k, TOP:TOP + 1, cols]
            send[t, 1, k:k + 1, :] = buf[t % 2, k, TOP + rows - 1:TOP + rows, cols]

        @pl.when(me > 0)
        def _():
            rim_copy(send, recv, ssem, rsem, t, 0).start()

        @pl.when(me < strips - 1)
        def _():
            rim_copy(send, recv, ssem, rsem, t, 1).start()

    def take_rims(buf, send, recv, ssem, rsem, t):
        def own(side):
            at = TOP if side == 0 else TOP + rows - 1
            to = TOP - 1 if side == 0 else TOP + rows
            for k in range(types):
                buf[t % 2, k, to:to + 1, cols] = buf[t % 2, k, at:at + 1, cols]

        def got(side):
            c = rim_copy(send, recv, ssem, rsem, t, side)
            c.wait_send()
            pltpu.make_async_remote_copy(
                src_ref=send.at[t, side], dst_ref=recv.at[t, side],
                send_sem=ssem.at[t, side], recv_sem=rsem.at[t, side],
                device_id={"strip": me - 1 if side == 0 else me + 1}, device_id_type=MESH,
            ).wait_recv()
            to = TOP - 1 if side == 0 else TOP + rows
            for k in range(types):
                buf[t % 2, k, to:to + 1, cols] = recv[t, side, k:k + 1, :]

        pl.when(me > 0)(lambda: got(0))
        pl.when(me == 0)(lambda: own(0))
        pl.when(me < strips - 1)(lambda: got(1))
        pl.when(me == strips - 1)(lambda: own(1))

    def pad_cols(buf, b):
        for k in range(types):
            first = buf[b, k, inner, LANE:2 * LANE]
            last = buf[b, k, inner, width:width + LANE]
            buf[b, k, inner, 0:LANE] = pltpu.roll(first, LANE - 1, 1)
            buf[b, k, inner, width + LANE:width + 2 * LANE] = pltpu.roll(last, 1, 1)

    def crowd_of(t, initial):
        b = t % 2

        @pl.loop(0, strips)
        def _(j):
            for q in range(per):
                start = pl.multiple_of(j * cw + q * LANE, LANE)
                at = pl.ds(pl.multiple_of(start + LANE, LANE), LANE)
                total = None
                if not initial:
                    keep = keep_map[:, pl.ds(start, LANE)]
                    ids = dst_map[:, pl.ds(start, LANE)]
                    slot = jnp.maximum(ids, 0)
                    landed = ids >= 0
                for k in range(types):
                    v = m_buf[b, k, inner, at]
                    if not initial:
                        if landings == 8:
                            add = jnp.concatenate([
                                jnp.take_along_axis(out_recv[t - 1, k], slot[r:r + 8], axis=0, mode="promise_in_bounds")
                                for r in range(0, rows, 8)
                            ], axis=0)
                            add = jnp.where(landed, add, 0.0)
                        else:
                            add = jnp.zeros_like(v)
                            for l in range(landings):
                                add = jnp.where(ids == l, out_recv[t - 1, k, l:l + 1, :], add)
                        v = v * keep + add
                        m_buf[b, k, inner, at] = v
                    term = tw_ref[k] * v
                    total = term if total is None else total + term
                if t < SUBSTEPS:
                    crowd_send[t, j, :, q * LANE:(q + 1) * LANE] = total.astype(jnp.bfloat16)

    def send_crowd(t):
        to_all(lambda d: crowd_send.at[t, d], crowd_recv.at[t], c_ssem.at[t], c_rsem.at[t])
        crowd_recv[t, me] = crowd_send[t, me]

    def mix(t):
        from_all(lambda d: crowd_send.at[t, d], crowd_recv.at[t], c_ssem.at[t], c_rsem.at[t])
        crowd = crowd_recv[t].reshape(strips * rows, cw)

        mixed = jnp.dot(rk[...].reshape(strips * rows, -1), crowd, preferred_element_type=jnp.float32)
        mix_send[t] = mixed.astype(jnp.bfloat16).reshape(strips, rows, cw)

        to_all(lambda d: mix_send.at[t, d], mix_recv.at[t], x_ssem.at[t], x_rsem.at[t])
        mix_recv[t, me] = mix_send[t, me]

    def add_potential(t):
        b = (t + 1) % 2
        from_all(lambda d: mix_send.at[t, d], mix_recv.at[t], x_ssem.at[t], x_rsem.at[t])
        step = 2 * LANE

        @pl.loop(0, width // step)
        def _(n):
            start = pl.multiple_of(n * step, step)
            acc = None
            for s in range(strips):
                d = jnp.dot(mix_recv[t, s], ck[s * cw:(s + 1) * cw, pl.ds(start, step)], preferred_element_type=jnp.float32)
                acc = d if acc is None else acc + d
            at = pl.ds(pl.multiple_of(start + LANE, LANE), step)
            for k in range(types):
                u_buf[b, k, inner, at] = u_buf[b, k, inner, at] + (time_step * cc_ref[k]) * acc

    def stencil(t, chunks):
        b, nb = t % 2, (t + 1) % 2

        @pl.loop(0, types * (width // BLOCK))
        def _(i):
            k = lax.div(i, width // BLOCK)
            start = pl.multiple_of(lax.rem(i, width // BLOCK) * BLOCK, BLOCK)
            wide = pl.ds(start, BLOCK + 2 * LANE)
            mid = pl.ds(pl.multiple_of(start + LANE, LANE), BLOCK)
            fac = drain_fac[k, :, pl.ds(start, BLOCK)]
            rew = reward[k, :, pl.ds(start, BLOCK)]
            for r in chunks:
                lo = TOP + 8 * r
                mw = m_buf[b, k, lo:lo + 8, wide]
                uw = u_buf[b, k, lo:lo + 8, wide]
                span = BLOCK + 2 * LANE
                m = mw[:, LANE:-LANE]
                u = uw[:, LANE:-LANE]
                ml = pltpu.roll(mw, 1, 1)[:, LANE:-LANE]
                mr = pltpu.roll(mw, span - 1, 1)[:, LANE:-LANE]
                ul = pltpu.roll(uw, 1, 1)[:, LANE:-LANE]
                ur = pltpu.roll(uw, span - 1, 1)[:, LANE:-LANE]
                mu = m_buf[b, k, lo - 1:lo + 7, mid]
                md = m_buf[b, k, lo + 1:lo + 9, mid]
                uu = u_buf[b, k, lo - 1:lo + 7, mid]
                ud = u_buf[b, k, lo + 1:lo + 9, mid]
                low = u - 2.0 * viscosity
                flux = None
                rise = None
                for mn, un in ((mu, uu), (md, ud), (ml, ul), (mr, ur)):
                    p = un - low
                    flux = mn * p if flux is None else flux + mn * p
                    rise = p if rise is None else rise + p
                gr = ud - uu
                gc = ur - ul
                drained = ((1.0 - 8.0 * viscosity * time_step) * m + (0.5 * time_step) * (flux + m * rise)) * fac
                m_buf[nb, k, lo:lo + 8, mid] = drained
                u_buf[nb, k, lo:lo + 8, mid] = u + (time_step * viscosity) * rise - (0.125 * time_step) * (gr * gr + gc * gc) - rew
                for q in range(BLOCK // LANE):
                    faces[(lax.div(start, LANE) + q) * (rows // 8) + r, k] = drained[:, q * LANE:(q + 1) * LANE]

    def out_copy(t):
        return pltpu.make_async_remote_copy(
            src_ref=out_send.at[t], dst_ref=out_recv.at[t],
            send_sem=o_ssem.at[t], recv_sem=o_rsem.at[t],
            device_id={"floor": floor - 1}, device_id_type=MESH,
        )

    def stairs(t):
        nb = (t + 1) % 2
        for l in range(landings):
            row = lm_ref[floor, l, 1]
            group = lax.div(row, 8)
            hit = eight + 8 * group == row
            face = faces[lm_ref[floor, l, 0] * (rows // 8) + group]
            out_send[t, :, l, :] = stair_rate * jnp.sum(jnp.where(hit, face, 0.0), axis=1)

        @pl.when(floor > 0)
        def _():
            out_copy(t).start()

    def stairs_in(t):
        @pl.when(floor > 0)
        def _():
            out_copy(t).wait_send()

        @pl.when(floor < floors - 1)
        def _():
            out_copy(t).wait_recv()

        @pl.when(floor == floors - 1)
        def _():
            out_recv[t] = jnp.zeros_like(out_recv[t])

    hm = (hm_send, hm_recv, hm_ssem, hm_rsem)
    hu = (hu_send, hu_recv, hu_ssem, hu_rsem)

    load_m.wait()
    crowd_of(0, True)
    send_crowd(0)
    send_rims(m_buf, *hm, 0)
    load_u.wait()
    send_rims(u_buf, *hu, 0)
    to_all(lambda d: rk_ref, rk, rk_ssem, rk_rsem)
    rk[me] = rk_ref[...]

    above = jnp.minimum(floor + 1, floors - 1)
    for tile in range(TILES):
        kind = et_ref[0, tile]
        here = slice(tile * tile_cols, (tile + 1) * tile_cols)
        for k in range(types):
            hit = jnp.where(kind == k, 1.0, 0.0).astype(jnp.float32)
            drain_fac[k, :, here] = jnp.full((8, tile_cols), 1.0 - ed_ref[k] * hit, jnp.float32)
            reward[k, :, here] = jnp.full((8, tile_cols), time_step * exit_reward * hit + 8.0 * viscosity * viscosity * time_step, jnp.float32)

    eight = lax.broadcasted_iota(jnp.int32, (types, 8, LANE), 1)
    row_at = lax.broadcasted_iota(jnp.int32, (rows, LANE), 0)

    @pl.loop(0, TILES)
    def _(tile):
        keep = jnp.ones((rows, LANE), jnp.float32)
        ids = jnp.full((rows, LANE), -1, jnp.int32)
        for l in range(landings):
            src_row = jnp.where(lm_ref[floor, l, 0] == tile, lm_ref[floor, l, 1], -1)
            dst_row = jnp.where(lm_ref[above, l, 2] == tile, lm_ref[above, l, 3], -1)
            keep = jnp.where(row_at == src_row, 1.0 - stair_rate, keep)
            ids = jnp.where(row_at == dst_row, l, ids)
        at = pl.ds(pl.multiple_of(tile * LANE, LANE), LANE)
        keep_map[:, at] = keep
        dst_map[:, at] = ids

    for t in range(SUBSTEPS):
        if t > 0:
            if t == 1:
                load_ck.wait()
            add_potential(t - 1)
            send_rims(u_buf, *hu, t)
        pad_cols(m_buf, t % 2)
        pad_cols(u_buf, t % 2)
        stencil(t, range(1, rows // 8 - 1))
        if t == 0:
            from_all(lambda d: rk_ref, rk, rk_ssem, rk_rsem)
        mix(t)
        take_rims(m_buf, *hm, t)
        take_rims(u_buf, *hu, t)
        stencil(t, (0, rows // 8 - 1))
        stairs(t)
        stairs_in(t)
        crowd_of(t + 1, False)
        if t + 1 < SUBSTEPS:
            send_crowd(t + 1)
            send_rims(m_buf, *hm, t + 1)
    last = SUBSTEPS % 2
    save_m = pltpu.make_async_copy(m_buf.at[last, :, inner, cols], dens_out.at[0], store_sem.at[0])
    save_m.start()
    add_potential(SUBSTEPS - 1)
    save_u = pltpu.make_async_copy(u_buf.at[last, :, inner, cols], val_out.at[0], store_sem.at[1])
    save_u.start()
    save_m.wait()
    save_u.wait()


def solution(mesh):
    strips = mesh.shape["strip"]
    floors = mesh.shape["floor"]

    def local(density, value_field, row_kernel, column_kernel, type_weight, crowd_cost, exit_drain, exit_type, landing_map):
        _, types, rows, width = density.shape
        landings = landing_map.shape[1]
        depth = row_kernel.shape[1]
        cw = width // strips
        n = SUBSTEPS
        any_spec = pl.BlockSpec(memory_space=pl.ANY)
        vmem = pl.BlockSpec(memory_space=pltpu.VMEM)
        smem = pl.BlockSpec(memory_space=pltpu.SMEM)
        f32, bf16 = jnp.float32, jnp.bfloat16
        dma = pltpu.SemaphoreType.DMA
        return pl.pallas_call(
            functools.partial(kernel, strips, floors, landings, types, rows, width),
            out_shape=(
                jax.ShapeDtypeStruct(density.shape, f32),
                jax.ShapeDtypeStruct(value_field.shape, f32),
            ),
            in_specs=[any_spec, any_spec, vmem, any_spec, smem, smem, smem, smem, smem],
            out_specs=(any_spec, any_spec),
            scratch_shapes=[
                pltpu.VMEM((2, types, rows + 2 * TOP, width + 2 * LANE), f32),
                pltpu.VMEM((2, types, rows + 2 * TOP, width + 2 * LANE), f32),
                pltpu.VMEM(column_kernel.shape, bf16),
                pltpu.VMEM((strips, rows, depth), bf16),
                pltpu.VMEM((n, strips, rows, cw), bf16),
                pltpu.VMEM((n, strips, rows, cw), bf16),
                pltpu.VMEM((n, strips, rows, cw), bf16),
                pltpu.VMEM((n, strips, rows, cw), bf16),
                pltpu.VMEM((n, 2, types, width), f32),
                pltpu.VMEM((n, 2, types, width), f32),
                pltpu.VMEM((n, 2, types, width), f32),
                pltpu.VMEM((n, 2, types, width), f32),
                pltpu.VMEM((n, types, landings, LANE), f32),
                pltpu.VMEM((n, types, landings, LANE), f32),
                pltpu.VMEM((types, 8, width), f32),
                pltpu.VMEM((types, 8, width), f32),
                pltpu.VMEM((rows, width), f32),
                pltpu.VMEM((rows, width), jnp.int32),
                pltpu.VMEM((width // LANE * (rows // 8), types, 8, LANE), f32),
                dma((3,)),
                dma((2,)),
                dma((strips,)),
                dma((strips,)),
                dma((n, strips)),
                dma((n, strips)),
                dma((n, strips)),
                dma((n, strips)),
                dma((n, 2)),
                dma((n, 2)),
                dma((n, 2)),
                dma((n, 2)),
                dma((n,)),
                dma((n,)),
            ],
            compiler_params=pltpu.CompilerParams(
                collective_id=0, has_side_effects=True, vmem_limit_bytes=52 * 1024 * 1024
            ),
        )(density, value_field, row_kernel, column_kernel, type_weight, crowd_cost, exit_drain, exit_type, landing_map)

    placed = (
        P("floor", None, "strip", None),
        P("floor", None, "strip", None),
        P("strip", None),
        P(),
        P(),
        P(),
        P(),
        P("floor", "strip"),
        P(None, "strip", None),
    )
    return jax.shard_map(
        local,
        mesh=mesh,
        in_specs=placed,
        out_specs=(P("floor", None, "strip", None), P("floor", None, "strip", None)),
        check_vma=False,
    )
```
